256 devices in a mesh: dom: 32 (over x, z_hi, core), src: 8 (over z_lo, y).
Axes of the slice: x: 4, y: 4, z: 8 (z_hi: 4, z_lo: 2; z = z_hi * 2 + z_lo), core: 2. Of those that a mesh axis runs over, the one named last changes fastest.
Arguments:
- features: float32 [65536, 256], P(('dom', 'src')), may hold values from -6 to 6
- w_self: float32 [256, 256], replicated, may hold values from -0.375 to 0.375
- w_neigh: float32 [256, 256], replicated, may hold values from -2 to 2
- bias: float32 [256], replicated, may hold values from -3 to 3
- tile_counts: int32 [4096, 128, 128], P(('dom', 'src')), may hold values 0 or 1
- tile_src: int32 [4096], P(('dom', 'src')), may hold values from 0 to 1
- hub_counts: int32 [65536, 1024], P('dom', 'src'), may hold values 0 or 1
- hub_rows: int32 [1024], P('src'), may hold values from 0 to 255
- halo_send: int32 [8192, 128], P(('dom', 'src')), may hold values from 0 to 255
- halo_dest: int32 [8192, 128], P(('dom', 'src')), may hold values from 0 to 2047
- cotangent: float32 [65536, 256], P(('dom', 'src')), may hold values from -6 to 6
Outputs:
- output: float32 [65536, 256], P(('dom', 'src'))
- grad_features: float32 [65536, 256], P(('dom', 'src'))
- grad_self: float32 [256, 256], replicated
- grad_neigh: float32 [256, 256], replicated
- grad_bias: float32 [256], replicated
The draws below stay inside these ranges and needn't reach their ends.
All inputs are finite; a program needn't handle non-finite values. No bound on the sum of `tile_counts` or of `hub_counts` on one device may be relied on, other than what follows from the above.
Results may differ from the reference program's by a relative error of at most 0.033.
Values sent between devices are 32-bit elements; how exact they have to be, the bound alone decides.
A program may use at most 64 MiB of HBM per device.

```python
import math
import jax
import jax.numpy as jnp
import numpy as np
from jax import lax

FEAT = 256
ROWS_DEV = 256
BLK = 128
HALO = 128
HUB_DEV = 128
PART_ROWS = 2048
NBLK = 16
NODES = 65536
N_DOM = 32
N_SRC = 8
DEVICES = 256


def set_ends(values, stream_key, smallest, largest):
    dims = values.shape
    index_at = [jax.random.randint(jax.random.fold_in(stream_key, axis), (), 0, dims[axis]) for axis in range(len(dims))]
    values = values.at[tuple(index_at)].set(smallest)
    longest = dims.index(max(dims))
    index_at[longest] = (index_at[longest] + 1) % dims[longest]
    return values.at[tuple(index_at)].set(largest)


def level_of(own_key, extent, split, low, top_value):
    level = 1.0
    for dim, blocks in split:
        heights = jax.random.uniform(jax.random.fold_in(jax.random.fold_in(own_key, 6), dim), (blocks,), jnp.float32, low / len(split), top_value / len(split))
        level = level * jnp.repeat(jnp.exp(heights), extent[dim] // blocks).reshape((-1,) + (1,) * (len(extent) - 1 - dim))
    return level


def cumulative_ranks(number_of, slope):
    weights = [(1 << 20) // math.isqrt(grade ** slope) + 1 for grade in range(1, number_of + 1)]
    scale = 1 + sum(weights) // (1 << 30)
    return np.cumsum(np.array([max(1, weight // scale) for weight in weights]))


def skewed_ids(key, extent, count, lean):
    listing = cumulative_ranks(count, lean)
    pick = jax.random.randint(jax.random.fold_in(key, 1), extent, 0, int(listing[count - 1]))
    standing = jnp.searchsorted(jnp.asarray(listing, jnp.int32), pick, side="right")
    return jax.random.permutation(jax.random.fold_in(key, 2), count)[standing].astype(jnp.int32)


def noise(own_key, shape, scale, most, cuts=(), kind=jnp.bfloat16):
    entries = jax.random.normal(own_key, shape, jnp.float32) * scale
    if len(cuts) > 0:
        entries = level_of(own_key, shape, cuts, -0.22, 0.18) * entries
    return jnp.clip(entries, min=-most, max=most).astype(kind)


def setup_inputs(seed: int = 0) -> dict:
    splits = jax.random.split(jax.random.key(seed), 12)
    features = noise(splits[0], (NODES, FEAT), 1.0, 6.0, ((0, 256),), jnp.float32)
    w_self = noise(splits[1], (FEAT, FEAT), FEAT ** -0.5, 0.375, (), jnp.float32)
    w_neigh = noise(splits[2], (FEAT, FEAT), (max(FEAT // 32, 1)) ** -0.5, 2.0, (), jnp.float32)
    bias = noise(splits[3], (FEAT,), 0.5, 3.0, (), jnp.float32)
    tile_counts = set_ends((jax.random.randint(splits[4], (DEVICES * NBLK, BLK, BLK), 0, 4) < 1).astype(jnp.int32), jax.random.fold_in(splits[4], 1), 0, 1)
    tile_src = set_ends(jax.random.randint(splits[5], (DEVICES * NBLK,), 0, ROWS_DEV // BLK), jax.random.fold_in(splits[5], 1), 0, (ROWS_DEV // BLK) - 1).astype(jnp.int32)
    hub_counts = set_ends((jax.random.randint(splits[6], (N_DOM * PART_ROWS, N_SRC * HUB_DEV), 0, 32) < 1).astype(jnp.int32), jax.random.fold_in(splits[6], 1), 0, 1)
    hub_rows = set_ends(jax.random.randint(splits[7], (N_SRC * HUB_DEV,), 0, ROWS_DEV), jax.random.fold_in(splits[7], 1), 0, ROWS_DEV - 1).astype(jnp.int32)
    halo_send = set_ends(jax.random.randint(splits[8], (DEVICES * N_DOM, HALO), 0, ROWS_DEV), jax.random.fold_in(splits[8], 1), 0, ROWS_DEV - 1).astype(jnp.int32)
    halo_dest = set_ends(skewed_ids(splits[9], (DEVICES * N_DOM, HALO), PART_ROWS, 2), jax.random.fold_in(splits[9], 3), 0, PART_ROWS - 1).astype(jnp.int32)
    cotangent = noise(splits[10], (NODES, FEAT), 1.0, 6.0, ((0, 256),), jnp.float32)
    return dict(features=features, w_self=w_self, w_neigh=w_neigh, bias=bias, tile_counts=tile_counts, tile_src=tile_src, hub_counts=hub_counts, hub_rows=hub_rows, halo_send=halo_send, halo_dest=halo_dest, cotangent=cotangent)


HIGH = lax.Precision.HIGHEST

def forward(features, w_self, w_neigh, bias, tile_counts, tile_src, hub_counts, hub_rows, halo_send, halo_dest):
    width = features.shape[1]
    cube = features.reshape(N_DOM, N_SRC, ROWS_DEV, width)
    panel = cube[0][jnp.arange(N_SRC)[:, None], hub_rows.reshape(N_SRC, HUB_DEV)].reshape(N_SRC * HUB_DEV, width)
    counts = tile_counts.reshape(N_DOM, N_SRC, NBLK, BLK, BLK)
    sources = tile_src.reshape(N_DOM, N_SRC, NBLK)
    sends = halo_send.reshape(N_DOM, N_SRC, N_DOM, HALO)
    dests = halo_dest.reshape(N_DOM, N_SRC, N_DOM, HALO)
    hubs = hub_counts.reshape(N_DOM, PART_ROWS, N_SRC * HUB_DEV)

    def one_part(part):
        sums = jnp.zeros((PART_ROWS, width), jnp.float32)
        degree = jnp.zeros((PART_ROWS,), jnp.float32)
        for source in range(N_SRC):
            blocks = cube[part, source].reshape(ROWS_DEV // BLK, BLK, width)
            chosen = blocks[sources[part, source]]
            weights = counts[part, source].astype(jnp.float32)
            sums = sums + jnp.einsum('bij,bjf->bif', weights, chosen, precision=HIGH).reshape(PART_ROWS, width)
            degree = degree + lax.optimization_barrier(jnp.sum(weights, axis=2)).reshape(PART_ROWS)
            received = cube[:, source][jnp.arange(N_DOM)[:, None], sends[:, source, part]]
            target = dests[part, source].reshape(-1)
            sums = sums.at[target].add(received.reshape(-1, width))
            degree = degree.at[target].add(jnp.ones(target.shape, jnp.float32))
        hub_weights = hubs[part].astype(jnp.float32)
        sums = sums + jnp.dot(hub_weights, panel, precision=HIGH)
        degree = degree + lax.optimization_barrier(jnp.sum(hub_weights, axis=1))
        return sums / (1.0 + degree)[:, None]
    agg = lax.map(one_part, jnp.arange(N_DOM)).reshape(features.shape)
    z = jnp.dot(features, w_self, precision=HIGH) + jnp.dot(agg, w_neigh, precision=HIGH) + bias
    y = jnp.maximum(z, 0.0)
    return y * lax.rsqrt(lax.optimization_barrier(jnp.mean(y * y, axis=1, keepdims=True)) + 1e-05)

def reference(features, w_self, w_neigh, bias, tile_counts, tile_src, hub_counts, hub_rows, halo_send, halo_dest, cotangent):

    def layer(feats, wa, wb, shift):
        return forward(feats, wa, wb, shift, tile_counts, tile_src, hub_counts, hub_rows, halo_send, halo_dest)
    output, pull = jax.vjp(layer, features, w_self, w_neigh, bias)
    grad_features, grad_self, grad_neigh, grad_bias = pull(cotangent)
    factor = 1.0 / jnp.sqrt(jnp.float32(features.shape[0]))
    return (output, grad_features, grad_self * factor, grad_neigh * factor, grad_bias * factor)
```

```python
import functools

import jax
import jax.numpy as jnp
from jax import lax
from jax.experimental import pallas as pl
from jax.experimental.pallas import tpu as pltpu
from jax.sharding import PartitionSpec as P

HIGH = lax.Precision.HIGHEST
MESH = pl.DeviceIdType.MESH
F32 = jnp.float32
BF16 = jnp.bfloat16
ROWS = 256
WID = 256
BLK = 128
PAY = ROWS + 16
HALF = PAY // 2
NQ = 32
NS = 8
DEG = ROWS + 8
CHUNK = 72
VMEM_LIMIT = 60 * 1024 * 1024


def coords():
    d = lax.axis_index("dom")
    s = lax.axis_index("src")
    return d, s, d // 8, (d // 2) % 4, d % 2


def dom_of(x, z, c):
    return x * 8 + z * 2 + c


def remote(src, dst, ssem, rsem, d, s):
    return pltpu.make_async_remote_copy(
        src_ref=src, dst_ref=dst, send_sem=ssem, recv_sem=rsem, device_id=(d, s), device_id_type=MESH
    )


def greet(peers):
    barrier = pltpu.get_barrier_semaphore()
    for d, s in peers:
        pl.semaphore_signal(barrier, inc=1, device_id=(d, s), device_id_type=MESH)
    pl.semaphore_wait(barrier, len(peers))


def split3(v):
    hi = v.astype(BF16)
    rest = v - hi.astype(F32)
    mid = rest.astype(BF16)
    low = (rest - mid.astype(F32)).astype(BF16)
    return hi, mid, low


def dot(a, b):
    return jnp.dot(a, b, preferred_element_type=F32)


def columns_of(row):
    return jnp.transpose(jnp.broadcast_to(row, (BLK, BLK)))


def pick_rows(row, width):
    col = columns_of(row)
    lane = lax.broadcasted_iota(jnp.int32, (BLK, BLK), 1).astype(row.dtype)
    parts = [jnp.where(col == lane + k * BLK, 1.0, 0.0).astype(BF16) for k in range(width // BLK)]
    return jnp.concatenate(parts, axis=1)


def forward_kernel(
    pay_ref, counts_ref, tsrc_ref, hub_ref, hubrow_ref, dest_ref,
    part_ref, sends_ref, local_ref,
    buf, gsc, dts, cnt,
    zsf, zrf, zsh, zrh, xsf, xrf, xsh, xrh, cs, cr, own_sem,
):
    d, s, x, z, c = coords()
    xp, xm, zp, zm = (x + 1) % 4, (x + 3) % 4, (z + 1) % 4, (z + 3) % 4
    x2, z2 = (x + 2) % 4, (z + 2) % 4
    dxp, dxm = dom_of(xp, z, c), dom_of(xm, z, c)
    dzp, dzm = dom_of(x, zp, c), dom_of(x, zm, c)
    dcore = dom_of(x, z, 1 - c)
    groups = (z, zm, zp, z2)

    def slot(cc, zz, xx):
        return (cc * 4 + zz) * 4 + xx

    greet([(dxp, s), (dxm, s), (dzp, s), (dzm, s), (dcore, s)])
    me = slot(c, z, x)
    pending = []

    def send(src, dst, ssem, rsem, dd):
        cp = remote(src, dst, ssem, rsem, dd, s)
        cp.start()
        pending.append(cp)

    def full(i):
        return buf.at[i]

    def top(i):
        return buf.at[i, pl.ds(0, HALF)]

    def bottom(i):
        return buf.at[i, pl.ds(HALF, HALF)]

    def arrived(ref, rsem):
        remote(ref, ref, own_sem, rsem, dcore, s).wait_recv()

    send(pay_ref, full(me), xsf.at[0, 0], xrf.at[0, 0], dxp)
    send(pay_ref, full(me), xsf.at[0, 1], xrf.at[0, 1], dxm)
    send(pay_ref, full(me), zsf.at[0], zrf.at[0], dzp)
    send(pay_ref, full(me), zsf.at[1], zrf.at[1], dzm)
    send(pay_ref, full(me), cs.at[0, 0], cr.at[0, 0], dcore)
    mine = pltpu.make_async_copy(pay_ref, full(me), own_sem)
    mine.start()

    def send_x(g):
        i = slot(c, groups[g], x)
        send(full(i), full(i), xsf.at[g, 0], xrf.at[g, 0], dxp)
        send(full(i), full(i), xsf.at[g, 1], xrf.at[g, 1], dxm)
        send(full(i), full(i), cs.at[g, 0], cr.at[g, 0], dcore)

    def forward_x(g):
        zz = groups[g]
        il, ir = slot(c, zz, xm), slot(c, zz, xp)
        arrived(full(il), xrf.at[g, 0])
        send(top(il), top(il), xsh.at[g, 0], xrh.at[g, 0], dxp)
        send(full(il), full(il), cs.at[g, 1], cr.at[g, 1], dcore)
        arrived(full(ir), xrf.at[g, 1])
        send(bottom(ir), bottom(ir), xsh.at[g, 1], xrh.at[g, 1], dxm)
        send(full(ir), full(ir), cs.at[g, 2], cr.at[g, 2], dcore)

    def finish_x(g):
        i = slot(c, groups[g], x2)
        arrived(top(i), xrh.at[g, 0])
        arrived(bottom(i), xrh.at[g, 1])
        send(full(i), full(i), cs.at[g, 3], cr.at[g, 3], dcore)

    def finish_core(g):
        zz = groups[g]
        for k, xx in enumerate((x, xm, xp, x2)):
            arrived(full(slot(1 - c, zz, xx)), cr.at[g, k])

    for b in range(16):
        w = counts_ref[b].astype(F32)
        first = jnp.where(tsrc_ref[b] == 0, 1.0, 0.0)
        rows = pl.ds(b * BLK, BLK)
        local_ref[rows, 0:BLK] = (w * first).astype(BF16)
        local_ref[rows, BLK : 2 * BLK] = (w * (1.0 - first)).astype(BF16)
        h = hub_ref[rows, :].astype(F32)
        local_ref[rows, 2 * BLK : 3 * BLK] = h.astype(BF16)
        cnt[rows, :] = w + h

    hi, mid, low = split3(pay_ref[0:ROWS, :])

    def local_step(m, carry):
        rows = pl.ds(pl.multiple_of(m * 512, 512), 512)
        t = local_ref[rows, 0:ROWS]
        acc = dot(t, hi) + dot(t, mid) + dot(t, low)
        part_ref[2 * m, 0:ROWS, :] = acc[0:ROWS]
        part_ref[2 * m + 1, 0:ROWS, :] = acc[ROWS:]
        return carry

    lax.fori_loop(0, 4, local_step, 0)
    mine.wait()

    def select(g):
        zz = groups[g]

        def step(k, carry):
            i = slot(k // 4, zz, k % 4)
            row = buf[i, pl.ds(ROWS + d % 16, 1), :]
            row = jnp.where(d >= 16, row[:, BLK:], row[:, :BLK])
            sends_ref[pl.ds(i, 1), :] = row
            onehot = pick_rows(row, ROWS)
            rows = pl.ds(pl.multiple_of(k * BLK, BLK), BLK)
            for n, piece in enumerate(split3(buf[i, 0:ROWS, :])):
                gsc[n, rows, :] = dot(onehot, piece).astype(BF16)
            return carry

        lax.fori_loop(0, 8, step, 0)

    def scatter(g):
        zz = groups[g]

        def step(m, carry):
            base = pl.multiple_of(m * 512, 512)
            rows = pl.ds(base, 512)
            row_id = lax.broadcasted_iota(jnp.int32, (512, BLK), 0) + m * 512
            total = cnt[rows, :]
            for k in range(8):
                q = dom_of(k % 4, zz, k // 4)
                hit = jnp.where(row_id == dest_ref[pl.ds(q, 1), :], 1.0, 0.0)
                total = total + hit
                dts[:, k * BLK : (k + 1) * BLK] = hit.astype(BF16)
            cnt[rows, :] = total
            t = dts[...]
            acc = dot(t, gsc[0, 0:1024]) + dot(t, gsc[1, 0:1024]) + dot(t, gsc[2, 0:1024])
            if g == 3:
                h = local_ref[rows, 2 * BLK : 3 * BLK]
                for n in range(3):
                    acc = acc + dot(h, gsc[n, 1024 : 1024 + BLK])
            part_ref[2 * m, 0:ROWS, :] += acc[0:ROWS]
            part_ref[2 * m + 1, 0:ROWS, :] += acc[ROWS:]
            return carry

        lax.fori_loop(0, 4, step, 0)

    forward_x(0)
    il, ir = slot(c, zm, x), slot(c, zp, x)
    arrived(full(il), zrf.at[0])
    send(top(il), top(il), zsh.at[0], zrh.at[0], dzp)
    send_x(1)
    arrived(full(ir), zrf.at[1])
    send(bottom(ir), bottom(ir), zsh.at[1], zrh.at[1], dzm)
    send_x(2)
    finish_x(0)
    far = slot(c, z2, x)
    arrived(top(far), zrh.at[0])
    arrived(bottom(far), zrh.at[1])
    send_x(3)
    finish_core(0)
    forward_x(1)
    select(0)
    scatter(0)
    forward_x(2)
    finish_x(1)
    finish_core(1)
    select(1)
    forward_x(3)
    scatter(1)
    finish_x(2)
    finish_core(2)
    select(2)
    scatter(2)
    finish_x(3)
    finish_core(3)
    select(3)
    hubhot = pick_rows(hubrow_ref[...], ROWS)
    for n, piece in enumerate(split3(buf[0, 0:ROWS, :])):
        gsc[n, 1024 : 1024 + BLK, :] = dot(hubhot, piece).astype(BF16)
    scatter(3)

    def degree_step(b, carry):
        block = cnt[pl.ds(pl.multiple_of(b * ROWS, ROWS), ROWS), :]
        row = jnp.sum(jnp.transpose(block), axis=0, keepdims=True)
        part_ref[b, ROWS:DEG, :] = jnp.broadcast_to(row, (8, ROWS))
        return carry

    lax.fori_loop(0, NS, degree_step, 0)
    for cp in pending:
        cp.wait_send()


def layer_kernel(
    part_ref, feat_ref, ws_ref, wn_ref, bias_ref, cot_ref,
    out_ref, dall_ref, dself_ref, grads_ref,
    got, dgot, dmine, s1, r1, s2, r2, own_sem,
):
    d, s, x, z, c = coords()
    peers = [(s + k) % NS for k in range(1, NS)]
    greet([(d, p) for p in peers])
    pending = []
    for k, p in enumerate(peers):
        cp = remote(part_ref.at[p], got.at[s], s1.at[k], r1.at[s], d, p)
        cp.start()
        pending.append(cp)
    feat = feat_ref[...]
    zself = jnp.dot(feat, ws_ref[...], precision=HIGH, preferred_element_type=F32) + bias_ref[...]
    feat_t = jnp.transpose(feat)
    total = part_ref[s]
    for k in range(1, NS):
        q = (s + NS - k) % NS
        remote(got.at[q], got.at[q], own_sem, r1.at[q], d, peers[0]).wait_recv()
        total = total + got[q]
    scale = 1.0 / (1.0 + total[ROWS : ROWS + 1, :])
    scale = jnp.transpose(jnp.broadcast_to(scale, (BLK, ROWS)))
    scale = jnp.concatenate([scale, scale], axis=1)
    agg = total[0:ROWS] * scale
    zz = zself + jnp.dot(agg, wn_ref[...], precision=HIGH, preferred_element_type=F32)
    y = jnp.maximum(zz, 0.0)
    r = lax.rsqrt(jnp.mean(y * y, axis=1, keepdims=True) + 1e-05)
    cot = cot_ref[...]
    out_ref[...] = y * r
    inner = jnp.sum(cot * y, axis=1, keepdims=True) * (1.0 / WID)
    dy = cot * r - y * (r * r * r * inner)
    dz = dy * jnp.where(zz > 0.0, 1.0, jnp.where(zz == 0.0, 0.5, 0.0))
    contract = (((1,), (1,)), ((), ()))
    dd = lax.dot_general(dz, wn_ref[...], contract, precision=HIGH, preferred_element_type=F32) * scale
    dmine[...] = dd
    for k, p in enumerate(peers):
        cp = remote(dmine, dgot.at[s], s2.at[k], r2.at[s], d, p)
        cp.start()
        pending.append(cp)
    dall_ref[s] = dd
    dself_ref[...] = lax.dot_general(dz, ws_ref[...], contract, precision=HIGH, preferred_element_type=F32)
    gs = jnp.dot(feat_t, dz, precision=HIGH, preferred_element_type=F32)
    gn = jnp.dot(jnp.transpose(agg), dz, precision=HIGH, preferred_element_type=F32)
    gb = jnp.sum(dz, axis=0, keepdims=True)
    for k in range(4):
        grads_ref[k, 0:64, :] = gs[k * 64 : (k + 1) * 64]
        grads_ref[4 + k, 0:64, :] = gn[k * 64 : (k + 1) * 64]
    for k in range(NS):
        grads_ref[k, 64:CHUNK, :] = jnp.broadcast_to(gb, (8, WID))
    for k in range(1, NS):
        q = (s + NS - k) % NS
        remote(dgot.at[q], dgot.at[q], own_sem, r2.at[q], d, peers[0]).wait_recv()
        dall_ref[q] = dgot[q]
    for cp in pending:
        cp.wait_send()


def backward_kernel(
    dall_ref, dself_ref, sends_ref, dest_ref, local_ref, hubrow_ref, grads_ref,
    gfeat_ref, gout_ref,
    contrib, crecv, xh, xf, zh, zf, dsplit, dhot, hubg, wgot, w1, w2, wcore, wx, w3, wz, w4, wall,
    csem, crsem, xsh, xrh, xsf, xrf, zsh, zrh, zsf, zrf,
    ws1, wr1, wcs, wcr, wxs, wxr, wzs, wzr, was, war, own_sem,
):
    d, s, x, z, c = coords()
    xp, xm, x2 = (x + 1) % 4, (x + 3) % 4, (x + 2) % 4
    zp, zm, z2 = (z + 1) % 4, (z + 3) % 4, (z + 2) % 4
    dxp, dxm, dx2 = dom_of(xp, z, c), dom_of(xm, z, c), dom_of(x2, z, c)
    dzp, dzm, dz2 = dom_of(x, zp, c), dom_of(x, zm, c), dom_of(x, z2, c)
    dcore = dom_of(x, z, 1 - c)
    speers = [(s + k) % NS for k in range(1, NS)]
    groups = (z2, zp, zm, z)
    greet(
        [(dxp, s), (dxm, s), (dx2, s), (dzp, s), (dzm, s), (dz2, s), (dcore, s)]
        + [(d, p) for p in speers]
    )
    pending = []

    def send(src, dst, ssem, rsem, dd, ss):
        cp = remote(src, dst, ssem, rsem, dd, ss)
        cp.start()
        pending.append(cp)

    def arrived(ref, rsem):
        remote(ref, ref, own_sem, rsem, dcore, s).wait_recv()

    def slot(cc, zz, xx):
        return (cc * 4 + zz) * 4 + xx

    for k, p in enumerate(speers):
        send(grads_ref.at[p], wgot.at[s], ws1.at[k], wr1.at[s], d, p)

    for b in range(NS):
        v = dall_ref[b]
        hi = v.astype(BF16)
        dsplit[0, b * ROWS : (b + 1) * ROWS, :] = hi
        dsplit[1, b * ROWS : (b + 1) * ROWS, :] = (v - hi.astype(F32)).astype(BF16)

    first = (((0,), (0,)), ((), ()))

    def back(cols):
        w = local_ref[:, cols]
        return lax.dot_general(w, dsplit[0], first, preferred_element_type=F32) + lax.dot_general(
            w, dsplit[1], first, preferred_element_type=F32
        )

    hubrow = hubrow_ref[...]
    row_id = lax.broadcasted_iota(jnp.int32, (ROWS, BLK), 0)
    hubhot = jnp.where(row_id == hubrow, 1.0, 0.0).astype(BF16)
    hg = back(slice(2 * BLK, 3 * BLK))
    hub_hi = hg.astype(BF16)
    hub_lo = (hg - hub_hi.astype(F32)).astype(BF16)
    hubg[...] = dot(hubhot, hub_hi) + dot(hubhot, hub_lo)

    def compute(zz, cc):
        for k in range(4):
            q = dom_of(k, zz, cc)
            dhot[k * BLK : (k + 1) * BLK, :] = pick_rows(dest_ref[pl.ds(q, 1), :], NS * ROWS)
        t = dhot[...]
        h_hi = dot(t, dsplit[0]).astype(BF16)
        h_lo = dot(t, dsplit[1]).astype(BF16)
        for k in range(4):
            i = slot(cc, zz, k)
            hot = jnp.where(row_id.astype(F32) == sends_ref[pl.ds(i, 1), :], 1.0, 0.0).astype(BF16)
            rows = slice(k * BLK, (k + 1) * BLK)
            contrib[i] = dot(hot, h_hi[rows]) + dot(hot, h_lo[rows])

    def add_hub():
        contrib[0] += hubg[...]

    H = ROWS // 2

    def core_send(g):
        i = slot(1 - c, groups[g], 0)
        send(contrib.at[pl.ds(i, 4)], crecv.at[g], csem.at[g], crsem.at[g], dcore, s)

    def x_first(g):
        i = slot(c, groups[g], 0)
        arrived(crecv.at[g], crsem.at[g])
        far = i + x2
        contrib[far] += crecv[g, x2]
        send(contrib.at[far, pl.ds(0, H)], xh.at[g, 0], xsh.at[g, 0], xrh.at[g, 0], dxp, s)
        send(contrib.at[far, pl.ds(H, H)], xh.at[g, 1], xsh.at[g, 1], xrh.at[g, 1], dxm, s)
        for xx in (xp, xm, x):
            contrib[i + xx] += crecv[g, xx]

    def x_second(g):
        i = slot(c, groups[g], 0)
        arrived(xh.at[g, 0], xrh.at[g, 0])
        contrib[i + xp, 0:H, :] += xh[g, 0]
        send(contrib.at[i + xp], xf.at[g, 0], xsf.at[g, 0], xrf.at[g, 0], dxp, s)
        arrived(xh.at[g, 1], xrh.at[g, 1])
        contrib[i + xm, H:ROWS, :] += xh[g, 1]
        send(contrib.at[i + xm], xf.at[g, 1], xsf.at[g, 1], xrf.at[g, 1], dxm, s)

    def x_last(g):
        i = slot(c, groups[g], x)
        arrived(xf.at[g, 0], xrf.at[g, 0])
        arrived(xf.at[g, 1], xrf.at[g, 1])
        contrib[i] += xf[g, 0] + xf[g, 1]
        return i

    def produce(g, hub):
        zz = groups[g]

        def step(k, carry):
            cc = jnp.where(k == 0, 1 - c, c)
            compute(zz, cc)
            return carry

        lax.fori_loop(0, 2, step, 0)
        i = slot(0, zz, 0)
        contrib[i] += jnp.where(zz == 0, 1.0, 0.0) * hubg[...]
        core_send(g)

    produce(0, False)

    x_first(0)
    produce(1, False)
    x_second(0)

    wt = grads_ref[s]
    for k in range(1, NS):
        q = (s + NS - k) % NS
        arrived(wgot.at[q], wr1.at[q])
        wt = wt + wgot[q]
    w1[...] = wt
    send(w1, wcore, wcs, wcr, dcore, s)

    x_first(1)
    produce(2, False)
    x_second(1)
    i = x_last(0)
    send(contrib.at[i, pl.ds(0, H)], zh.at[0], zsh.at[0], zrh.at[0], dzp, s)
    send(contrib.at[i, pl.ds(H, H)], zh.at[1], zsh.at[1], zrh.at[1], dzm, s)

    arrived(wcore, wcr)
    wt = w1[...] + wcore[...]
    w2[...] = wt
    wx[x] = wt
    for k, dd in enumerate((dxp, dxm, dx2)):
        send(w2, wx.at[x], wxs.at[k], wxr.at[x], dd, s)

    x_first(2)
    produce(3, False)
    x_second(2)
    i = x_last(1)
    arrived(zh.at[0], zrh.at[0])
    contrib[i, 0:H, :] += zh[0]
    send(contrib.at[i], zf.at[0], zsf.at[0], zrf.at[0], dzp, s)

    x_first(3)
    x_second(3)
    i = x_last(2)
    arrived(zh.at[1], zrh.at[1])
    contrib[i, H:ROWS, :] += zh[1]
    send(contrib.at[i], zf.at[1], zsf.at[1], zrf.at[1], dzm, s)

    for xx in (xp, xm, x2):
        arrived(wx.at[xx], wxr.at[xx])
    wt = (wx[0] + wx[1]) + (wx[2] + wx[3])
    w3[...] = wt
    wz[z] = wt
    for k, dd in enumerate((dzp, dzm, dz2)):
        send(w3, wz.at[z], wzs.at[k], wzr.at[z], dd, s)

    total = back(slice(0, 2 * BLK)) + dself_ref[...]

    for q in (zp, zm, z2):
        arrived(wz.at[q], wzr.at[q])
    wt = (wz[0] + wz[1]) + (wz[2] + wz[3])
    w4[...] = wt
    for k, p in enumerate(speers):
        send(w4, wall.at[s], was.at[k], war.at[s], d, p)

    i = x_last(3)
    total = total + contrib[i]
    arrived(zf.at[0], zrf.at[0])
    arrived(zf.at[1], zrf.at[1])
    gfeat_ref[...] = total + (zf[0] + zf[1])

    factor = 1.0 / 256.0
    gout_ref[s] = w4[...] * factor
    for k in range(1, NS):
        q = (s + NS - k) % NS
        arrived(wall.at[q], war.at[q])
        gout_ref[q] = wall[q] * factor
    for cp in pending:
        cp.wait_send()


def vspec():
    return pl.BlockSpec(memory_space=pltpu.VMEM)


def params(cid):
    return pltpu.CompilerParams(collective_id=cid, has_side_effects=True, vmem_limit_bytes=VMEM_LIMIT)


def dma(*shape):
    return pltpu.SemaphoreType.DMA(shape) if shape else pltpu.SemaphoreType.DMA


def body(
    features, w_self, w_neigh, bias, tile_counts, tile_src, hub_counts, hub_rows, halo_send, halo_dest, cotangent
):
    sds = jax.ShapeDtypeStruct
    vm = pltpu.VMEM
    packed = halo_send.astype(F32).reshape(2, 16, BLK).transpose(1, 0, 2).reshape(16, WID)
    payload = jnp.concatenate([features, packed], axis=0)
    hubrow = hub_rows.reshape(1, BLK)
    part, sends, local = pl.pallas_call(
        forward_kernel,
        name="forward_sums",
        out_shape=(sds((NS, DEG, WID), F32), sds((NQ, BLK), F32), sds((NS * ROWS, 3 * BLK), BF16)),
        in_specs=[vspec(), vspec(), pl.BlockSpec(memory_space=pltpu.SMEM), vspec(), vspec(), vspec()],
        out_specs=(vspec(),) * 3,
        scratch_shapes=[
            vm((NQ, PAY, WID), F32),
            vm((3, 1024 + BLK, WID), BF16),
            vm((512, 1024), BF16),
            vm((NS * ROWS, BLK), F32),
            dma(2), dma(2), dma(2), dma(2),
            dma(4, 2), dma(4, 2), dma(4, 2), dma(4, 2),
            dma(4, 4), dma(4, 4), dma(),
        ],
        compiler_params=params(0),
    )(payload, tile_counts, tile_src, hub_counts, hubrow, halo_dest)
    output, d_all, d_self, grads = pl.pallas_call(
        layer_kernel,
        name="dense_layer",
        out_shape=(
            sds((ROWS, WID), F32), sds((NS, ROWS, WID), F32), sds((ROWS, WID), F32), sds((NS, CHUNK, WID), F32),
        ),
        in_specs=[vspec()] * 6,
        out_specs=(vspec(),) * 4,
        scratch_shapes=[
            vm((NS, DEG, WID), F32),
            vm((NS, ROWS, WID), F32),
            vm((ROWS, WID), F32),
            dma(NS - 1), dma(NS), dma(NS - 1), dma(NS), dma(),
        ],
        compiler_params=params(1),
    )(part, features, w_self, w_neigh, bias.reshape(1, WID), cotangent)
    w = lambda *lead: vm((*lead, CHUNK, WID), F32)
    grad_features, gout = pl.pallas_call(
        backward_kernel,
        name="backward_sums",
        out_shape=(sds((ROWS, WID), F32), sds((NS, CHUNK, WID), F32)),
        in_specs=[vspec()] * 7,
        out_specs=(vspec(),) * 2,
        scratch_shapes=[
            vm((NQ, ROWS, WID), F32),
            vm((4, 4, ROWS, WID), F32),
            vm((4, 2, ROWS // 2, WID), F32),
            vm((4, 2, ROWS, WID), F32),
            vm((2, ROWS // 2, WID), F32),
            vm((2, ROWS, WID), F32),
            vm((2, NS * ROWS, WID), BF16),
            vm((512, NS * ROWS), BF16),
            vm((ROWS, WID), F32),
            w(NS), w(), w(), w(), w(4), w(), w(4), w(), w(NS),
            dma(4), dma(4), dma(4, 2), dma(4, 2), dma(4, 2), dma(4, 2),
            dma(2), dma(2), dma(2), dma(2),
            dma(NS - 1), dma(NS), dma(), dma(), dma(3), dma(4), dma(3), dma(4),
            dma(NS - 1), dma(NS), dma(),
        ],
        compiler_params=params(2),
    )(d_all, d_self, sends, halo_dest, local, hubrow, grads)
    grad_self = gout[0:4, 0:64].reshape(WID, WID)
    grad_neigh = gout[4:8, 0:64].reshape(WID, WID)
    return output, grad_features, grad_self, grad_neigh, gout[0, 64]


def solution(mesh):
    return jax.shard_map(
        body,
        mesh=mesh,
        in_specs=(
            P(("dom", "src"), None),
            P(),
            P(),
            P(),
            P(("dom", "src"), None, None),
            P(("dom", "src")),
            P("dom", "src"),
            P("src"),
            P(("dom", "src"), None),
            P(("dom", "src"), None),
            P(("dom", "src"), None),
        ),
        out_specs=(P(("dom", "src"), None), P(("dom", "src"), None), P(), P(), P()),
        check_vma=False,
    )
```

```python
import functools

import jax
import jax.numpy as jnp
from jax import lax
from jax.experimental import pallas as pl
from jax.experimental.pallas import tpu as pltpu
from jax.sharding import PartitionSpec as P

HIGH = lax.Precision.HIGHEST
MESH = pl.DeviceIdType.MESH
F32 = jnp.float32
BF16 = jnp.bfloat16
ROWS = 256
WID = 256
BLK = 128
PAY = ROWS + 16
HALF = PAY // 2
NQ = 32
NS = 8
DEG = ROWS + 8
CHUNK = 72
VMEM_LIMIT = 67043328


def coords():
    d = lax.axis_index("dom")
    s = lax.axis_index("src")
    return d, s, d // 8, (d // 2) % 4, d % 2


def dom_of(x, z, c):
    return x * 8 + z * 2 + c


def remote(src, dst, ssem, rsem, d, s):
    return pltpu.make_async_remote_copy(
        src_ref=src, dst_ref=dst, send_sem=ssem, recv_sem=rsem, device_id=(d, s), device_id_type=MESH
    )


def greet(peers):
    barrier = pltpu.get_barrier_semaphore()
    for d, s in peers:
        pl.semaphore_signal(barrier, inc=1, device_id=(d, s), device_id_type=MESH)
    pl.semaphore_wait(barrier, len(peers))


def split3(v):
    hi = v.astype(BF16)
    rest = v - hi.astype(F32)
    mid = rest.astype(BF16)
    low = (rest - mid.astype(F32)).astype(BF16)
    return hi, mid, low


def dot(a, b):
    return jnp.dot(a, b, preferred_element_type=F32)


def columns_of(row):
    return jnp.transpose(jnp.broadcast_to(row, (BLK, BLK)))


def pick_rows(row, width):
    col = columns_of(row)
    lane = lax.broadcasted_iota(jnp.int32, (BLK, BLK), 1).astype(row.dtype)
    parts = [jnp.where(col == lane + k * BLK, 1.0, 0.0).astype(BF16) for k in range(width // BLK)]
    return jnp.concatenate(parts, axis=1)


def layer_kernel(
    feat_ref, hsend_ref, counts_ref, tsrc_ref, hub_ref, hubrow_ref, dest_ref,
    ws_ref, wn_ref, bias_ref, cot_ref,
    out_ref, gfeat_ref, gall_ref, gbias_ref,
    buf, gsc, dts, cnt, acc, local, local_t, sends, destp,
    zsf, zrf, zsh, zrh, xsf, xrf, xsh, xrh, cs, cr,
    part_a, part_b, a1, a2, a3, b1, b2, b3,
    a1s, a1r, a2s, a2r, a3s, a3r, b1s, b1r, b2s, b2r, b3s, b3r,
    ga, gb, gas, gar, gbs, gbr, gbhr,
    dself, grads, dsplit, dhot, hubg,
    crecv, hx, fx, hz, fz,
    csem, crsem, hxs, hxr, fxs, fxr, hzs, hzr, fzs, fzr,
    wgot, w1, w2, wcore, wx, w3, wz, w4, wall,
    ws1, wr1, wcs, wcr, wxs, wxr, wzs, wzr, was, war, own_sem,
):
    d, s, x, z, c = coords()
    zl, y = s // 4, s % 4
    xp, xm, x2 = (x + 1) % 4, (x + 3) % 4, (x + 2) % 4
    zp, zm, z2 = (z + 1) % 4, (z + 3) % 4, (z + 2) % 4
    yp, ym, y2 = (y + 1) % 4, (y + 3) % 4, (y + 2) % 4
    zo = 1 - zl
    dxp, dxm, dx2 = dom_of(xp, z, c), dom_of(xm, z, c), dom_of(x2, z, c)
    dzp, dzm, dz2 = dom_of(x, zp, c), dom_of(x, zm, c), dom_of(x, z2, c)
    dcore = dom_of(x, z, 1 - c)
    syp, sym, szo = zl * 4 + yp, zl * 4 + ym, zo * 4 + y
    speers = [(s + k) % NS for k in range(1, NS)]
    H = ROWS // 2

    def slot(cc, zz, xx):
        return (cc * 4 + zz) * 4 + xx

    me = slot(c, z, x)
    buf[me, 0:ROWS, :] = feat_ref[...]
    buf[me, ROWS:PAY, 0:BLK] = hsend_ref[0:16, :].astype(F32)
    buf[me, ROWS:PAY, BLK:WID] = hsend_ref[16:32, :].astype(F32)
    greet(
        [(dxp, s), (dxm, s), (dx2, s), (dzp, s), (dzm, s), (dz2, s), (dcore, s)]
        + [(d, p) for p in speers]
    )
    pending = []

    def send(src, dst, ssem, rsem, dd, ss):
        cp = remote(src, dst, ssem, rsem, dd, ss)
        cp.start()
        pending.append(cp)

    def arrived(ref, rsem):
        remote(ref, ref, own_sem, rsem, dcore, s).wait_recv()

    def drain():
        for cp in pending:
            cp.wait_send()
        pending.clear()

    groups = (z, zm, zp, z2)

    def full(i):
        return buf.at[i]

    def top(i):
        return buf.at[i, pl.ds(0, HALF)]

    def bottom(i):
        return buf.at[i, pl.ds(HALF, HALF)]

    def send_x(g):
        i = slot(c, groups[g], x)
        send(full(i), full(i), xsf.at[g, 0], xrf.at[g, 0], dxp, s)
        send(full(i), full(i), xsf.at[g, 1], xrf.at[g, 1], dxm, s)

    def send_core(g, k, i):
        send(full(i), full(i), cs.at[g, k], cr.at[g, k], dcore, s)

    def forward_x(g):
        zz = groups[g]
        il, ir = slot(c, zz, xm), slot(c, zz, xp)
        arrived(full(il), xrf.at[g, 0])
        send(top(il), top(il), xsh.at[g, 0], xrh.at[g, 0], dxp, s)
        send_core(g, 1, il)
        arrived(full(ir), xrf.at[g, 1])
        send(bottom(ir), bottom(ir), xsh.at[g, 1], xrh.at[g, 1], dxm, s)
        send_core(g, 2, ir)

    def finish_x(g):
        i = slot(c, groups[g], x2)
        arrived(top(i), xrh.at[g, 0])
        arrived(bottom(i), xrh.at[g, 1])
        send_core(g, 3, i)

    def finish_core(g):
        for k, xx in enumerate((x, xm, xp, x2)):
            arrived(full(slot(1 - c, groups[g], xx)), cr.at[g, k])

    send_x(0)
    send(full(me), full(me), zsf.at[0], zrf.at[0], dzp, s)
    send(full(me), full(me), zsf.at[1], zrf.at[1], dzm, s)
    send_core(0, 0, me)

    dest = dest_ref[...]
    blk = dest // ROWS
    destp[...] = ((blk % 4) * 2 + blk // 4) * ROWS + dest % ROWS

    def spot(b):
        k = b // 2
        return ((k % 4) * 2 + k // 4) * ROWS + (b % 2) * BLK

    for b in range(16):
        w = counts_ref[b].astype(F32)
        first = jnp.where(tsrc_ref[b] == 0, 1.0, 0.0)
        rows = slice(spot(b), spot(b) + BLK)
        local[rows, 0:BLK] = (w * first).astype(BF16)
        local[rows, BLK : 2 * BLK] = (w * (1.0 - first)).astype(BF16)
        h = hub_ref[b * BLK : (b + 1) * BLK, :].astype(F32)
        local[rows, 2 * BLK : 3 * BLK] = h.astype(BF16)
        cnt[rows, :] = w + h

    def hot_step(n, carry):
        m, i = n // 8, n % 8
        rows = pl.ds(pl.multiple_of(m * 512, 512), 512)
        row_id = lax.broadcasted_iota(jnp.int32, (512, BLK), 0) + m * 512
        total = cnt[rows, :]
        for k in range(4):
            q = dom_of(k, i % 4, i // 4)
            hit = jnp.where(row_id == destp[pl.ds(q, 1), :], 1.0, 0.0)
            total = total + hit
            dts[i, rows, k * BLK : (k + 1) * BLK] = hit.astype(BF16)
        cnt[rows, :] = total
        return carry

    lax.fori_loop(0, 16, hot_step, 0)
    forward_x(0)

    hi, mid, low = split3(feat_ref[...])

    def local_step(m, carry):
        rows = pl.ds(pl.multiple_of(m * 512, 512), 512)
        t = local[rows, 0:ROWS]
        acc[rows, :] = dot(t, hi) + dot(t, mid) + dot(t, low)
        return carry

    def select(g):
        zz = groups[g]

        def step(k, carry):
            i = slot(k // 4, zz, k % 4)
            row = buf[i, pl.ds(ROWS + d % 16, 1), :]
            row = jnp.where(d >= 16, row[:, BLK:], row[:, :BLK])
            sends[pl.ds(i, 1), :] = row
            onehot = pick_rows(row, ROWS)
            rows = pl.ds(pl.multiple_of(k * BLK, BLK), BLK)
            for n, piece in enumerate(split3(buf[i, 0:ROWS, :])):
                gsc[n, rows, :] = dot(onehot, piece).astype(BF16)
            return carry

        lax.fori_loop(0, 8, step, 0)

    def spread(g, m):
        zz = groups[g]
        rows = pl.ds(pl.multiple_of(m * 512, 512), 512)
        v = acc[rows, :]
        for cc in range(2):
            t = dts[cc * 4 + zz, rows, :]
            for n in range(3):
                v = v + dot(t, gsc[n, cc * 512 : (cc + 1) * 512])
        return v

    def scatter(g):
        def step(m, carry):
            rows = pl.ds(pl.multiple_of(m * 512, 512), 512)
            acc[rows, :] = spread(g, m)
            return carry

        lax.fori_loop(0, 4, step, 0)

    il, ir = slot(c, zm, x), slot(c, zp, x)
    arrived(full(il), zrf.at[0])
    send(top(il), top(il), zsh.at[0], zrh.at[0], dzp, s)
    send_x(1)
    arrived(full(ir), zrf.at[1])
    send(bottom(ir), bottom(ir), zsh.at[1], zrh.at[1], dzm, s)
    send_x(2)
    finish_x(0)
    send_core(1, 0, il)
    send_core(2, 0, ir)
    lax.fori_loop(16, 32, hot_step, 0)
    lax.fori_loop(0, 4, local_step, 0)

    def degree_step(m, carry):
        for k in range(2):
            block = cnt[pl.ds(pl.multiple_of(m * 512 + k * ROWS, ROWS), ROWS), :]
            row = jnp.sum(jnp.transpose(block), axis=0, keepdims=True)
            part_a[m, k, ROWS:DEG, :] = jnp.broadcast_to(row[:, 0:BLK], (8, BLK))
            part_a[m, k, ROWS + 1 : ROWS + 2, :] = row[:, BLK:ROWS]
        return carry

    lax.fori_loop(0, 4, degree_step, 0)
    far = slot(c, z2, x)
    arrived(top(far), zrh.at[0])
    arrived(bottom(far), zrh.at[1])
    send_x(3)
    send_core(3, 0, far)
    finish_core(0)
    forward_x(1)
    forward_x(2)
    select(0)
    finish_x(1)
    finish_x(2)
    scatter(0)
    finish_core(1)
    select(1)
    scatter(1)
    forward_x(3)
    finish_core(2)
    select(2)
    scatter(2)
    hubhot = pick_rows(hubrow_ref[...], ROWS)

    def add_hub():
        for n, piece in enumerate(split3(buf[0, 0:ROWS, :])):
            gsc[n, 1024 : 1024 + BLK, :] = dot(hubhot, piece).astype(BF16)

    finish_x(3)
    zself = jnp.dot(feat_ref[...], ws_ref[...], precision=HIGH, preferred_element_type=F32) + bias_ref[...]
    dself[...] = zself
    finish_core(3)
    add_hub()
    select(3)

    def last(m):
        rows = pl.ds(pl.multiple_of(m * 512, 512), 512)
        v = spread(3, m)
        h = local[rows, 2 * BLK : 3 * BLK]
        for n in range(3):
            v = v + dot(h, gsc[n, 1024 : 1024 + BLK])
        for k in range(2):
            part_a[m, k, 0:ROWS, :] = v[k * ROWS : (k + 1) * ROWS, 0:BLK]
            part_b[k, m, :, :] = v[k * ROWS : (k + 1) * ROWS, BLK:WID]

    last(y2)
    send(part_a.at[y2, 0], a1.at[0], a1s.at[0], a1r.at[0], d, syp)
    send(part_a.at[y2, 1], a1.at[1], a1s.at[1], a1r.at[1], d, sym)
    send(part_b.at[zo, y2], b1.at[0], b1s.at[0], b1r.at[0], d, szo)
    last(yp)
    send(part_b.at[zo, yp], b1.at[1], b1s.at[1], b1r.at[1], d, szo)
    last(ym)
    send(part_b.at[zo, ym], b1.at[2], b1s.at[2], b1r.at[2], d, szo)
    arrived(a1.at[0], a1r.at[0])
    part_a[yp, 0, :, :] += a1[0]
    send(part_a.at[yp], a2.at[0], a2s.at[0], a2r.at[0], d, syp)
    arrived(a1.at[1], a1r.at[1])
    part_a[ym, 1, :, :] += a1[1]
    send(part_a.at[ym], a2.at[1], a2s.at[1], a2r.at[1], d, sym)
    last(y)
    send(part_b.at[zo, y], b1.at[3], b1s.at[3], b1r.at[3], d, szo)
    arrived(b1.at[0], b1r.at[0])
    part_b[zl, y2, :, :] += b1[0]
    send(part_b.at[zl, y2, pl.ds(0, H)], b2.at[0], b2s.at[0], b2r.at[0], d, syp)
    send(part_b.at[zl, y2, pl.ds(H, H)], b2.at[1], b2s.at[1], b2r.at[1], d, sym)
    arrived(a2.at[0], a2r.at[0])
    arrived(a2.at[1], a2r.at[1])
    part_a[y, :, :, :] += a2[0] + a2[1]
    send(part_a.at[y, zo], a3, a3s, a3r, d, szo)
    arrived(b1.at[1], b1r.at[1])
    part_b[zl, yp, :, :] += b1[1]
    arrived(b2.at[0], b2r.at[0])
    part_b[zl, yp, 0:H, :] += b2[0]
    send(part_b.at[zl, yp], b3.at[0], b3s.at[0], b3r.at[0], d, syp)
    arrived(b1.at[2], b1r.at[2])
    part_b[zl, ym, :, :] += b1[2]
    arrived(b2.at[1], b2r.at[1])
    part_b[zl, ym, H:ROWS, :] += b2[1]
    send(part_b.at[zl, ym], b3.at[1], b3s.at[1], b3r.at[1], d, sym)
    feat_t = jnp.transpose(feat_ref[...])
    arrived(b1.at[3], b1r.at[3])
    arrived(a3, a3r)
    tot_a = part_a[y, zl] + a3[...]
    arrived(b3.at[0], b3r.at[0])
    arrived(b3.at[1], b3r.at[1])
    tot_b = (part_b[zl, y] + b1[3]) + (b3[0] + b3[1])

    scale = 1.0 / (1.0 + jnp.concatenate([tot_a[ROWS : ROWS + 1], tot_a[ROWS + 1 : ROWS + 2]], axis=1))
    scale = jnp.transpose(jnp.broadcast_to(scale, (BLK, ROWS)))
    scale2 = jnp.concatenate([scale, scale], axis=1)
    agg = jnp.concatenate([tot_a[0:ROWS], tot_b], axis=1) * scale2
    zz = dself[...] + jnp.dot(agg, wn_ref[...], precision=HIGH, preferred_element_type=F32)
    yy = jnp.maximum(zz, 0.0)
    r = lax.rsqrt(jnp.mean(yy * yy, axis=1, keepdims=True) + 1e-05)
    cot = cot_ref[...]
    inner = jnp.sum(cot * yy, axis=1, keepdims=True) * (1.0 / WID)
    dy = cot * r - yy * (r * r * r * inner)
    dz = dy * jnp.where(zz > 0.0, 1.0, jnp.where(zz == 0.0, 0.5, 0.0))
    contract = (((1,), (1,)), ((), ()))
    dd = lax.dot_general(dz, wn_ref[...], contract, precision=HIGH, preferred_element_type=F32) * scale2
    ga[y, zl, :, :] = dd[:, 0:BLK]
    gb[zl, y, :, :] = dd[:, BLK:WID]

    def push_a(yy_, zz_, k):
        send(ga.at[yy_, zz_], ga.at[yy_, zz_], gas.at[k], gar.at[yy_, zz_], d, syp)
        send(ga.at[yy_, zz_], ga.at[yy_, zz_], gas.at[k + 1], gar.at[yy_, zz_], d, sym)

    def push_b(yy_, k):
        send(gb.at[zl, yy_], gb.at[zl, yy_], gbs.at[k], gbr.at[zl, yy_], d, szo)

    send(gb.at[zl, y], gb.at[zl, y], gbs.at[0], gbr.at[zl, y], d, syp)
    send(gb.at[zl, y], gb.at[zl, y], gbs.at[1], gbr.at[zl, y], d, sym)
    send(ga.at[y, zl], ga.at[y, zl], gas.at[0], gar.at[y, zl], d, szo)
    push_a(y, zl, 1)
    push_b(y, 2)
    out_ref[...] = yy * r
    drop = jnp.sum(dz, axis=0, keepdims=True)
    dself[...] = lax.dot_general(dz, ws_ref[...], contract, precision=HIGH, preferred_element_type=F32)
    arrived(ga.at[y, zo], gar.at[y, zo])
    push_a(y, zo, 3)
    gs = jnp.dot(feat_t, dz, precision=HIGH, preferred_element_type=F32)
    gn = jnp.dot(jnp.transpose(agg), dz, precision=HIGH, preferred_element_type=F32)
    for k in range(4):
        grads[k, 0:64, :] = gs[k * 64 : (k + 1) * 64]
        grads[4 + k, 0:64, :] = gn[k * 64 : (k + 1) * 64]
    for k in range(NS):
        grads[k, 64:CHUNK, :] = jnp.broadcast_to(drop, (8, WID))
    arrived(gb.at[zl, ym], gbr.at[zl, ym])
    send(gb.at[zl, ym, pl.ds(0, H)], gb.at[zl, ym, pl.ds(0, H)], gbs.at[3], gbhr.at[0], d, syp)
    push_b(ym, 4)
    arrived(gb.at[zl, yp], gbr.at[zl, yp])
    send(gb.at[zl, yp, pl.ds(H, H)], gb.at[zl, yp, pl.ds(H, H)], gbs.at[5], gbhr.at[1], d, sym)
    push_b(yp, 6)
    arrived(ga.at[ym, zl], gar.at[ym, zl])
    arrived(ga.at[yp, zl], gar.at[yp, zl])
    arrived(ga.at[ym, zo], gar.at[ym, zo])
    send(ga.at[ym, 0], ga.at[ym, 0], gas.at[5], gar.at[ym, 0], d, syp)
    arrived(ga.at[yp, zo], gar.at[yp, zo])
    send(ga.at[yp, 1], ga.at[yp, 1], gas.at[6], gar.at[yp, 1], d, sym)
    arrived(gb.at[zl, y2, pl.ds(0, H)], gbhr.at[0])
    arrived(gb.at[zl, y2, pl.ds(H, H)], gbhr.at[1])
    push_b(y2, 7)
    for k, p in enumerate(speers):
        send(grads.at[p], wgot.at[s], ws1.at[k], wr1.at[s], d, p)

    for b in range(16):
        w = jnp.transpose(counts_ref[b].astype(F32))
        first = jnp.where(tsrc_ref[b] == 0, 1.0, 0.0)
        cols = slice(spot(b), spot(b) + BLK)
        local_t[0:BLK, cols] = (w * first).astype(BF16)
        local_t[BLK : 2 * BLK, cols] = (w * (1.0 - first)).astype(BF16)
        h = jnp.transpose(hub_ref[b * BLK : (b + 1) * BLK, :].astype(F32))
        local_t[2 * BLK : 3 * BLK, cols] = h.astype(BF16)

    groups = (z2, zp, zm, z)

    def fill(g, h):
        cc = 1 - c if h == 0 else c

        def step(k, carry):
            q = dom_of(k, groups[g], cc)
            rows = pl.ds(pl.multiple_of(k * BLK, BLK), BLK)
            dhot[h, rows, :] = pick_rows(destp[pl.ds(q, 1), :], NS * ROWS)
            return carry

        lax.fori_loop(0, 4, step, 0)

    fill(0, 0)
    fill(0, 1)

    arrived(ga.at[y2, 0], gar.at[y2, 0])
    arrived(ga.at[y2, 1], gar.at[y2, 1])
    for q in (y, yp, ym, y2):
        arrived(gb.at[zo, q], gbr.at[zo, q])
    for k in range(NS):
        rows = slice(k * ROWS, (k + 1) * ROWS)
        for v, cols in ((ga[k // 2, k % 2], slice(0, BLK)), (gb[k % 2, k // 2], slice(BLK, WID))):
            hi = v.astype(BF16)
            dsplit[0, rows, cols] = hi
            dsplit[1, rows, cols] = (v - hi.astype(F32)).astype(BF16)
    drain()

    def back(rows):
        w = local_t[rows, :]
        return dot(w, dsplit[0]) + dot(w, dsplit[1])

    row_id = lax.broadcasted_iota(jnp.int32, (ROWS, BLK), 0)

    def contrib(i):
        return buf.at[i, pl.ds(0, ROWS)]

    def produce(g):
        gz = groups[g]
        for h in range(2):
            cc = 1 - c if h == 0 else c
            if g > 0:
                fill(g, h)
            t = dhot[h]
            h_hi = dot(t, dsplit[0]).astype(BF16)
            h_lo = dot(t, dsplit[1]).astype(BF16)
            for k in range(4):
                i = slot(cc, gz, k)
                hot = jnp.where(row_id.astype(F32) == sends[pl.ds(i, 1), :], 1.0, 0.0).astype(BF16)
                rows = slice(k * BLK, (k + 1) * BLK)
                v = dot(hot, h_hi[rows]) + dot(hot, h_lo[rows])
                if k == 0:
                    v = v + jnp.where(cc * 4 + gz == 0, 1.0, 0.0) * hubg[...]
                buf[i, 0:ROWS, :] = v
            if h == 0:
                i = slot(cc, gz, 0)
                send(buf.at[pl.ds(i, 4), pl.ds(0, ROWS)], crecv.at[g], csem.at[g], crsem.at[g], dcore, s)

    def x_first(g):
        i = slot(c, groups[g], 0)
        arrived(crecv.at[g], crsem.at[g])
        f = i + x2
        buf[f, 0:ROWS, :] += crecv[g, x2]
        send(buf.at[f, pl.ds(0, H)], hx.at[g, 0], hxs.at[g, 0], hxr.at[g, 0], dxp, s)
        send(buf.at[f, pl.ds(H, H)], hx.at[g, 1], hxs.at[g, 1], hxr.at[g, 1], dxm, s)
        for xx in (xp, xm, x):
            buf[i + xx, 0:ROWS, :] += crecv[g, xx]

    def x_second(g):
        i = slot(c, groups[g], 0)
        arrived(hx.at[g, 0], hxr.at[g, 0])
        buf[i + xp, 0:H, :] += hx[g, 0]
        send(contrib(i + xp), fx.at[g, 0], fxs.at[g, 0], fxr.at[g, 0], dxp, s)
        arrived(hx.at[g, 1], hxr.at[g, 1])
        buf[i + xm, H:ROWS, :] += hx[g, 1]
        send(contrib(i + xm), fx.at[g, 1], fxs.at[g, 1], fxr.at[g, 1], dxm, s)

    def x_last(g):
        i = slot(c, groups[g], x)
        arrived(fx.at[g, 0], fxr.at[g, 0])
        arrived(fx.at[g, 1], fxr.at[g, 1])
        buf[i, 0:ROWS, :] += fx[g, 0] + fx[g, 1]
        return i

    hubhot2 = jnp.where(row_id == hubrow_ref[...], 1.0, 0.0).astype(BF16)
    hg = back(slice(2 * BLK, 3 * BLK))
    hub_hi = hg.astype(BF16)
    hub_lo = (hg - hub_hi.astype(F32)).astype(BF16)
    hubg[...] = dot(hubhot2, hub_hi) + dot(hubhot2, hub_lo)
    produce(0)
    x_first(0)
    produce(1)
    x_first(1)
    x_second(0)
    wt = grads[s]
    for k in range(1, NS):
        q = (s + NS - k) % NS
        arrived(wgot.at[q], wr1.at[q])
        wt = wt + wgot[q]
    w1[...] = wt
    send(w1, wcore, wcs, wcr, dcore, s)
    produce(2)
    x_first(2)
    x_second(1)
    i = x_last(0)
    send(buf.at[i, pl.ds(0, H)], hz.at[0], hzs.at[0], hzr.at[0], dzp, s)
    send(buf.at[i, pl.ds(H, H)], hz.at[1], hzs.at[1], hzr.at[1], dzm, s)
    arrived(wcore, wcr)
    wt = w1[...] + wcore[...]
    w2[...] = wt
    wx[x] = wt
    produce(3)
    x_first(3)
    for k, dd_ in enumerate((dxp, dxm, dx2)):
        send(w2, wx.at[x], wxs.at[k], wxr.at[x], dd_, s)
    x_second(2)
    i = x_last(1)
    arrived(hz.at[0], hzr.at[0])
    buf[i, 0:H, :] += hz[0]
    send(contrib(i), fz.at[0], fzs.at[0], fzr.at[0], dzp, s)
    x_second(3)
    i = x_last(2)
    arrived(hz.at[1], hzr.at[1])
    buf[i, H:ROWS, :] += hz[1]
    send(contrib(i), fz.at[1], fzs.at[1], fzr.at[1], dzm, s)
    for xx in (xp, xm, x2):
        arrived(wx.at[xx], wxr.at[xx])
    wt = (wx[0] + wx[1]) + (wx[2] + wx[3])
    w3[...] = wt
    wz[z] = wt
    for k, dd_ in enumerate((dzp, dzm, dz2)):
        send(w3, wz.at[z], wzs.at[k], wzr.at[z], dd_, s)
    total = back(slice(0, 2 * BLK)) + dself[...]
    i = x_last(3)
    total = total + buf[i, 0:ROWS, :]
    for q in (zp, zm, z2):
        arrived(wz.at[q], wzr.at[q])
    wt = (wz[0] + wz[1]) + (wz[2] + wz[3])
    w4[...] = wt
    for k, p in enumerate(speers):
        send(w4, wall.at[s], was.at[k], war.at[s], d, p)
    arrived(fz.at[0], fzr.at[0])
    arrived(fz.at[1], fzr.at[1])
    gfeat_ref[...] = total + (fz[0] + fz[1])
    factor = 1.0 / 256.0
    wall[s] = wt
    for k in range(1, NS):
        q = (s + NS - k) % NS
        arrived(wall.at[q], war.at[q])
    for q in range(NS):
        gall_ref[q * 64 : (q + 1) * 64, :] = wall[q, 0:64, :] * factor
    gbias_ref[...] = wall[0, 64:CHUNK, :] * factor
    drain()


def vspec():
    return pl.BlockSpec(memory_space=pltpu.VMEM)


def dma(*shape):
    return pltpu.SemaphoreType.DMA(shape) if shape else pltpu.SemaphoreType.DMA


def body(
    features, w_self, w_neigh, bias, tile_counts, tile_src, hub_counts, hub_rows, halo_send, halo_dest, cotangent
):
    sds = jax.ShapeDtypeStruct
    vm = pltpu.VMEM
    w = lambda *lead: vm((*lead, CHUNK, WID), F32)
    H = ROWS // 2
    output, grad_features, gall, gbias = pl.pallas_call(
        layer_kernel,
        name="sage_layer",
        out_shape=(
            sds((ROWS, WID), F32), sds((ROWS, WID), F32), sds((2 * WID, WID), F32), sds((8, WID), F32),
        ),
        in_specs=[vspec()] * 3 + [pl.BlockSpec(memory_space=pltpu.SMEM)] + [vspec()] * 7,
        out_specs=(vspec(),) * 4,
        scratch_shapes=[
            vm((NQ, PAY, WID), F32),
            vm((3, 1024 + BLK, WID), BF16),
            vm((8, NS * ROWS, 512), BF16),
            vm((NS * ROWS, BLK), F32),
            vm((NS * ROWS, WID), F32),
            vm((NS * ROWS, 3 * BLK), BF16),
            vm((3 * BLK, NS * ROWS), BF16),
            vm((NQ, BLK), F32),
            vm((NQ, BLK), jnp.int32),
            dma(2), dma(2), dma(2), dma(2),
            dma(4, 2), dma(4, 2), dma(4, 2), dma(4, 2),
            dma(4, 4), dma(4, 4),
            vm((4, 2, DEG, BLK), F32),
            vm((2, 4, ROWS, BLK), F32),
            vm((2, DEG, BLK), F32),
            vm((2, 2, DEG, BLK), F32),
            vm((DEG, BLK), F32),
            vm((4, ROWS, BLK), F32),
            vm((2, H, BLK), F32),
            vm((2, ROWS, BLK), F32),
            dma(2), dma(2), dma(2), dma(2), dma(), dma(),
            dma(4), dma(4), dma(2), dma(2), dma(2), dma(2),
            vm((4, 2, ROWS, BLK), F32),
            vm((2, 4, ROWS, BLK), F32),
            dma(7), dma(4, 2), dma(8), dma(2, 4), dma(2),
            vm((ROWS, WID), F32),
            w(NS),
            vm((2, NS * ROWS, WID), BF16),
            vm((2, 512, NS * ROWS), BF16),
            vm((ROWS, WID), F32),
            vm((4, 4, ROWS, WID), F32),
            vm((4, 2, H, WID), F32),
            vm((4, 2, ROWS, WID), F32),
            vm((2, H, WID), F32),
            vm((2, ROWS, WID), F32),
            dma(4), dma(4), dma(4, 2), dma(4, 2), dma(4, 2), dma(4, 2),
            dma(2), dma(2), dma(2), dma(2),
            w(NS), w(), w(), w(), w(4), w(), w(4), w(), w(NS),
            dma(NS - 1), dma(NS), dma(), dma(), dma(3), dma(4), dma(3), dma(4),
            dma(NS - 1), dma(NS), dma(),
        ],
        compiler_params=pltpu.CompilerParams(
            collective_id=0, has_side_effects=True, vmem_limit_bytes=VMEM_LIMIT
        ),
    )(
        features, halo_send, tile_counts, tile_src, hub_counts, hub_rows.reshape(1, BLK), halo_dest,
        w_self, w_neigh, bias.reshape(1, WID), cotangent,
    )
    return output, grad_features, gall[0:WID], gall[WID:], gbias[0]


def solution(mesh):
    return jax.shard_map(
        body,
        mesh=mesh,
        in_specs=(
            P(("dom", "src"), None),
            P(),
            P(),
            P(),
            P(("dom", "src"), None, None),
            P(("dom", "src")),
            P("dom", "src"),
            P("src"),
            P(("dom", "src"), None),
            P(("dom", "src"), None),
            P(("dom", "src"), None),
        ),
        out_specs=(P(("dom", "src"), None), P(("dom", "src"), None), P(), P(), P()),
        check_vma=False,
    )
```
